32 devices in a mesh: dp: 4 (over y, x), tensor: 8 (over z, core).
Axes of the slice: x: 2, y: 2, z: 4, core: 2. Of those that a mesh axis runs over, the one named last changes fastest.
Arguments:
- hidden_x: bfloat16 [32, 128, 16384], P('dp', None, 'tensor'), may hold values from -6 to 6
- gate_z: bfloat16 [32, 128, 16384], P('dp', None, 'tensor'), may hold values from -6 to 6
- conv_weight: float32 [4, 16384], P(None, 'tensor'), may hold values from -3 to 3
- conv_bias: float32 [16384], P('tensor'), may hold values from -0.5 to 0.5
- x_weight: bfloat16 [16384, 544], P('tensor'), may hold values from -0.046875 to 0.046875
- dt_weight: bfloat16 [512, 16384], P(None, 'tensor'), may hold values from -0.25 to 0.25
- dt_bias: float32 [16384], P('tensor'), may hold values from -6 to -2
- a_log: float32 [16, 16384], P(None, 'tensor'), may hold values from -2 to 2.7
- skip_gain: float32 [16384], P('tensor'), may hold values from 0.5 to 1.5
- ssm_cache: float32 [32, 16, 16384], P('dp', None, 'tensor'), may hold values from -6 to 6
- conv_cache: float32 [32, 3, 16384], P('dp', None, 'tensor'), may hold values from -6 to 6
- holder_of: int32 [32], replicated, may hold values from 0 to 3, as said below
- slot_of: int32 [32], replicated, may hold values from 0 to 7, as said below
Outputs:
- gated_out: bfloat16 [32, 128, 16384], P('dp', None, 'tensor')
- new_ssm: float32 [32, 16, 16384], P('dp', None, 'tensor')
- new_conv: float32 [32, 3, 16384], P('dp', None, 'tensor')
The draws below stay inside these ranges and needn't reach their ends.
Inputs may be any that keep to these rules, and one draw needn't show every extreme that they name: `holder_of`: requests 8 * g to 8 * g + 7 belong to dp group g. One holder serves at most 2 requests of one group, and in every group some holder serves exactly 2. `slot_of`: requests with the same holder have different slots.
All inputs are finite; a program needn't handle non-finite values.
Results may differ from the reference program's by a relative error of at most 0.0062.
Values may be sent and summed in bfloat16 or wider, within the bound.
A program may use at most 128 MiB of HBM per device.

```python
import jax
import jax.numpy as jnp
from jax import lax

INNER = 16384
DT_RANK = 512
STATE = 16
CONV = 4
TURN = 128
REQ_DEV = 8
CAP = 2
REQUESTS = 32
SLOTS = 8
N_DP = 4


def routing(key):
    candidates = N_DP * CAP
    noise_draw = jax.random.randint(jax.random.fold_in(key, 101), (N_DP, candidates), 0, 4096)
    hottest = jax.random.randint(jax.random.fold_in(key, 102), (), 0, N_DP)
    partners = jax.random.randint(jax.random.fold_in(key, 105), (N_DP,), 0, N_DP)
    owners = jnp.arange(candidates, dtype=jnp.int32) // CAP
    group_ids = jnp.arange(N_DP, dtype=jnp.int32)
    forced = (group_ids == (hottest + 1) % N_DP) | (group_ids == (hottest + N_DP // 2) % N_DP)
    targets = jnp.where(forced, hottest, partners)
    levels = jnp.where(owners[None, :] == targets[:, None], 2, 0) + jnp.where(owners[None, :] == group_ids[:, None], 1, 0)
    scores = levels * 4194304 + noise_draw * candidates + jnp.arange(candidates, dtype=jnp.int32)[None, :]
    unused, chosen = lax.top_k(scores, REQ_DEV)
    holders = (chosen // CAP).astype(jnp.int32)
    shuffle_scores = jax.random.randint(jax.random.fold_in(key, 103), (N_DP, REQ_DEV), 0, 4096) * REQ_DEV + jnp.arange(REQ_DEV, dtype=jnp.int32)[None, :]
    unused_two, order = lax.top_k(shuffle_scores, REQ_DEV)
    holders = jnp.take_along_axis(holders, order, axis=1)
    earlier = jnp.arange(REQ_DEV)[None, :] < jnp.arange(REQ_DEV)[:, None]
    same_holder = holders[:, :, None] == holders[:, None, :]
    rank_within = jnp.sum((same_holder & earlier[None, :, :]).astype(jnp.int32), axis=2)
    offsets = jax.random.randint(jax.random.fold_in(key, 104), (N_DP,), 0, SLOTS)
    slot_rows = (group_ids[:, None] * CAP + rank_within + offsets[holders]) % SLOTS
    return (holders.reshape(-1).astype(jnp.int32), slot_rows.reshape(-1).astype(jnp.int32))


def draw_holder_of(key, part):
    return routing(key)[0]


def draw_slot_of(key, part):
    return routing(key)[1]


def block_scale(own_key, shape, cuts, low, largest):
    loudness = 1.0
    for position, shards_of in cuts:
        draws = jax.random.uniform(jax.random.fold_in(jax.random.fold_in(own_key, 6), position), (shards_of,), jnp.float32, low / len(cuts), largest / len(cuts))
        loudness = loudness * jnp.repeat(jnp.exp(draws), shape[position] // shards_of).reshape((-1,) + (1,) * (len(shape) - 1 - position))
    return loudness


def scatter_about(rng, shape, width, most, pieces=(), held_as=jnp.bfloat16):
    loudness = block_scale(rng, shape, pieces, -0.22, 0.18) if pieces else 1.0
    values = jax.random.normal(rng, shape, jnp.float32) * width * loudness
    return jnp.minimum(jnp.maximum(values, -most), most).astype(held_as)


def setup_inputs(seed: int = 0) -> dict:
    streams_of = jax.random.split(jax.random.key(seed), 14)
    return {
        "hidden_x": scatter_about(streams_of[0], (REQUESTS, TURN, INNER), 1.0, 6.0, ((0, 4), (2, 8))),
        "gate_z": scatter_about(streams_of[1], (REQUESTS, TURN, INNER), 1.0, 6.0, ((0, 4), (2, 8))),
        "conv_weight": scatter_about(streams_of[2], (CONV, INNER), CONV ** -0.5, 3.0, ((1, 8),), jnp.float32),
        "conv_bias": jnp.clip(jax.random.uniform(streams_of[3], (INNER,), jnp.float32, -0.5, 0.5) * block_scale(streams_of[3], (INNER,), ((0, 8),), -0.4, 0.0), -0.5, 0.5),
        "x_weight": scatter_about(streams_of[4], (INNER, DT_RANK + 2 * STATE), INNER ** -0.5, 0.046875, ((0, 8),)),
        "dt_weight": scatter_about(streams_of[5], (DT_RANK, INNER), DT_RANK ** -0.5, 0.25, ((1, 8),)),
        "dt_bias": jnp.clip(-6.0 + 4.0 * jax.random.uniform(streams_of[6], (INNER,), jnp.float32) ** block_scale(streams_of[6], (INNER,), ((0, 8),), -0.2, 0.2), -6.0, -2.0),
        "a_log": jnp.clip(-2.0 + 4.7 * jax.random.uniform(streams_of[7], (STATE, INNER), jnp.float32) ** block_scale(streams_of[7], (STATE, INNER), ((1, 8),), -0.2, 0.2), -2.0, 2.7),
        "skip_gain": jnp.clip(0.5 + 1.0 * jax.random.uniform(streams_of[8], (INNER,), jnp.float32) ** block_scale(streams_of[8], (INNER,), ((0, 8),), -0.2, 0.2), 0.5, 1.5),
        "ssm_cache": scatter_about(streams_of[9], (SLOTS * N_DP, STATE, INNER), 1.0, 6.0, ((0, 4), (2, 8)), jnp.float32),
        "conv_cache": scatter_about(streams_of[10], (SLOTS * N_DP, CONV - 1, INNER), 1.0, 6.0, ((0, 4), (2, 8)), jnp.float32),
        "holder_of": draw_holder_of(jax.random.fold_in(streams_of[13], 71), 0),
        "slot_of": draw_slot_of(jax.random.fold_in(streams_of[13], 71), 0),
    }


EPSILON = 1e-06
NORM_FLOOR = 0.25

def normalize(projected, rank_width, state_width):
    dt_raw = projected[:, :rank_width]
    inject_raw = projected[:, rank_width:rank_width + state_width]
    readout_raw = projected[:, rank_width + state_width:]
    dt_norm = dt_raw * lax.rsqrt(lax.optimization_barrier(jnp.mean(dt_raw * dt_raw, axis=1, keepdims=True)) + EPSILON)
    inject_norm = inject_raw * lax.rsqrt(jnp.maximum(lax.optimization_barrier(jnp.mean(inject_raw * inject_raw, axis=1, keepdims=True)), NORM_FLOOR))
    readout_norm = readout_raw * lax.rsqrt(jnp.maximum(lax.optimization_barrier(jnp.mean(readout_raw * readout_raw, axis=1, keepdims=True)), NORM_FLOOR))
    joined = jnp.concatenate([inject_norm, readout_norm], axis=1)
    return (dt_norm.astype(jnp.bfloat16), joined.astype(jnp.bfloat16))

def convolve(hidden_rows, conv_start, conv_weight, conv_bias):
    turn_len = hidden_rows.shape[1]
    extended = jnp.concatenate([conv_start, hidden_rows.astype(jnp.float32)], axis=1)
    summed = jnp.zeros(hidden_rows.shape, jnp.float32) + conv_bias[None, None, :]
    for offset in range(conv_weight.shape[0]):
        summed = summed + extended[:, offset:offset + turn_len, :] * conv_weight[offset][None, None, :]
    return jax.nn.silu(summed).astype(jnp.bfloat16)

def advance(carried, decay_rate, dt_now, drive_now, inject_now, readout_now):
    carried = jnp.exp(dt_now[:, None, :] * decay_rate[None, :, :]) * carried + drive_now[:, None, :] * inject_now[:, :, None]
    return (carried, lax.optimization_barrier(jnp.sum(readout_now[:, :, None] * carried, axis=1)))

def reference(hidden_x, gate_z, conv_weight, conv_bias, x_weight, dt_weight, dt_bias, a_log, skip_gain, ssm_cache, conv_cache, holder_of, slot_of):
    where_at = (holder_of * SLOTS + slot_of).astype(jnp.int32)
    state_all = ssm_cache[where_at].reshape(N_DP, REQ_DEV, STATE, INNER)
    conv_all = conv_cache[where_at].reshape(N_DP, REQ_DEV, CONV - 1, INNER)
    grouped_x = hidden_x.reshape(N_DP, REQ_DEV, TURN, INNER)
    grouped_z = gate_z.reshape(N_DP, REQ_DEV, TURN, INNER)
    decay_rate = -jnp.exp(a_log)

    def one_group(inputs):
        group_x, group_z, conv_start, state_start = inputs
        conv_out = convolve(group_x, conv_start, conv_weight, conv_bias)
        flat_rows = conv_out.reshape(-1, INNER)
        projected = jnp.dot(flat_rows, x_weight, preferred_element_type=jnp.float32)
        dt_norm, bc_norm = normalize(projected, DT_RANK, STATE)
        dt_full = jax.nn.softplus(jnp.dot(dt_norm, dt_weight, preferred_element_type=jnp.float32) + dt_bias[None, :])
        dt_full = dt_full.reshape(group_x.shape)
        drive_full = dt_full * conv_out.astype(jnp.float32)
        bc_full = bc_norm.astype(jnp.float32).reshape(group_x.shape[0], group_x.shape[1], 2 * STATE)

        def stepper(carried, slices):
            dt_now, drive_now, inject_now, readout_now = slices
            return advance(carried, decay_rate, dt_now, drive_now, inject_now, readout_now)
        final_state, readout = lax.scan(stepper, state_start, (jnp.swapaxes(dt_full, 0, 1), jnp.swapaxes(drive_full, 0, 1), jnp.swapaxes(bc_full[:, :, :STATE], 0, 1), jnp.swapaxes(bc_full[:, :, STATE:], 0, 1)))
        readout = jnp.swapaxes(readout, 0, 1)
        gated = ((readout + skip_gain[None, None, :] * conv_out.astype(jnp.float32)) * jax.nn.silu(group_z.astype(jnp.float32))).astype(jnp.bfloat16)
        return (gated, final_state)
    gated, final_state = lax.map(one_group, (grouped_x, grouped_z, conv_all, state_all))
    gated_out = gated.reshape(REQUESTS, TURN, INNER)
    new_ssm = ssm_cache.at[where_at].set(final_state.reshape(REQUESTS, STATE, INNER))
    new_conv = conv_cache.at[where_at].set(hidden_x[:, TURN - (CONV - 1):, :].astype(jnp.float32))
    return (gated_out, new_ssm, new_conv)
```

```python
import functools

import jax
import jax.numpy as jnp
from jax import lax
from jax.experimental import pallas as pl
from jax.experimental.pallas import tpu as pltpu
from jax.sharding import PartitionSpec as P

EPSILON = 1e-06
NORM_FLOOR = 0.25
LOG2E = 1.4426950408889634
CHUNKS = 2
BLOCK = 256
LANES = 128


def normalize(projected, rank_width, state_width):
    dt_raw = projected[:, :rank_width]
    inject_raw = projected[:, rank_width : rank_width + state_width]
    readout_raw = projected[:, rank_width + state_width :]
    dt_norm = dt_raw * lax.rsqrt(jnp.mean(dt_raw * dt_raw, axis=1, keepdims=True) + EPSILON)
    inject_norm = inject_raw * lax.rsqrt(
        jnp.maximum(jnp.mean(inject_raw * inject_raw, axis=1, keepdims=True), NORM_FLOOR)
    )
    readout_norm = readout_raw * lax.rsqrt(
        jnp.maximum(jnp.mean(readout_raw * readout_raw, axis=1, keepdims=True), NORM_FLOOR)
    )
    return jnp.concatenate([dt_norm, inject_norm, readout_norm], axis=1).astype(jnp.bfloat16)


def conv_kernel(x_ref, start_ref, cw_ref, cb_ref, xw_ref, out_ref, proj_ref, ext):
    step = pl.program_id(0)
    requests, turn, width = x_ref.shape
    taps = cw_ref.shape[0]
    tile = 16
    ext[0 : taps - 1] = start_ref[...]

    def gather(i, _):
        t = pl.multiple_of(i * tile, tile)
        rows = x_ref[:, pl.ds(t, tile), :].astype(jnp.float32)
        ext[pl.ds(taps - 1 + t, tile)] = jnp.swapaxes(rows, 0, 1)
        return 0

    lax.fori_loop(0, turn // tile, gather, 0)
    weights = [cw_ref[j : j + 1, :][None] for j in range(taps)]
    bias = cb_ref[...][None]

    def convolve(i, _):
        t = i * tile
        total = ext[pl.ds(t, tile)] * weights[0] + bias
        for j in range(1, taps):
            total = total + ext[pl.ds(t + j, tile)] * weights[j]
        value = total / (1.0 + jnp.exp(-total))
        row = pl.multiple_of(t * requests, tile * requests)
        out_ref[pl.ds(row, tile * requests), :] = value.reshape(tile * requests, width).astype(
            jnp.bfloat16
        )
        return 0

    lax.fori_loop(0, turn // tile, convolve, 0)

    @pl.when(step == 0)
    def _():
        proj_ref[...] = jnp.dot(out_ref[...], xw_ref[...], preferred_element_type=jnp.float32)

    @pl.when(step > 0)
    def _():
        proj_ref[...] += jnp.dot(out_ref[...], xw_ref[...], preferred_element_type=jnp.float32)


def conv_project(chunk, turn, hidden_x, start, conv_weight, conv_bias, x_weight):
    requests, _, inner = hidden_x.shape
    taps = conv_weight.shape[0]
    cols = x_weight.shape[1]
    rows = requests * turn
    return pl.pallas_call(
        conv_kernel,
        grid=(inner // BLOCK,),
        in_specs=[
            pl.BlockSpec((requests, turn, BLOCK), lambda j: (0, chunk, j)),
            pl.BlockSpec((taps - 1, requests, BLOCK), lambda j: (0, 0, j)),
            pl.BlockSpec((taps, BLOCK), lambda j: (0, j)),
            pl.BlockSpec((1, BLOCK), lambda j: (0, j)),
            pl.BlockSpec((BLOCK, cols), lambda j: (j, 0)),
        ],
        out_specs=[
            pl.BlockSpec((rows, BLOCK), lambda j: (0, j)),
            pl.BlockSpec((rows, cols), lambda j: (0, 0)),
        ],
        out_shape=[
            jax.ShapeDtypeStruct((rows, inner), jnp.bfloat16),
            jax.ShapeDtypeStruct((rows, cols), jnp.float32),
        ],
        scratch_shapes=[pltpu.VMEM((turn + taps - 1, requests, BLOCK), jnp.float32)],
        compiler_params=pltpu.CompilerParams(vmem_limit_bytes=40 * 1024 * 1024),
        cost_estimate=pl.CostEstimate(
            flops=2 * rows * inner * cols,
            bytes_accessed=rows * inner * 4 + inner * cols * 2 + rows * cols * 4,
            transcendentals=2 * rows * inner,
        ),
    )(hidden_x, start, conv_weight, conv_bias.reshape(1, -1), x_weight)


def scan_kernel(
    aliased,
    norm_ref,
    x_ref,
    z_ref,
    dtw_ref,
    dtb_ref,
    alog_ref,
    skip_ref,
    state_ref,
    *rest,
):
    if aliased:
        rest = rest[1:]
    out_ref, final_ref, bc_s, dt_s, drive_s, y_s = rest
    step = pl.program_id(0)
    requests, turn, width = z_ref.shape
    states = alog_ref.shape[0]
    rank = dtw_ref.shape[0]
    rows = requests * turn
    tile = 128

    @pl.when(step == 0)
    def _():
        def spread(i, _):
            row = pl.multiple_of(i * 16, 16)
            both = norm_ref[pl.ds(row, 16), rank:].astype(jnp.float32)
            for half in range(16 // requests):
                part = both[half * requests : (half + 1) * requests]
                t = i * (16 // requests) + half
                for n in range(2 * states):
                    bc_s[t, n] = jnp.broadcast_to(part[:, n : n + 1], (requests, LANES))
            return 0

        lax.fori_loop(0, rows // 16, spread, 0)

    bias = dtb_ref[...]
    skip = skip_ref[...]

    def steps(i, _):
        row = pl.multiple_of(i * tile, tile)
        raw = jnp.dot(
            norm_ref[pl.ds(row, tile), :rank], dtw_ref[...], preferred_element_type=jnp.float32
        )
        raw = raw + bias
        dt = jnp.maximum(raw, 0.0) + jnp.log1p(jnp.exp(-jnp.abs(raw)))
        x = x_ref[pl.ds(row, tile), :].astype(jnp.float32)
        dt_s[pl.ds(row, tile), :] = dt
        drive_s[pl.ds(row, tile), :] = dt * x
        y_s[pl.ds(row, tile), :] = skip * x
        return 0

    lax.fori_loop(0, rows // tile, steps, 0)

    for part in range(width // LANES):
        lanes = slice(part * LANES, (part + 1) * LANES)
        rates = -jnp.exp(alog_ref[:, lanes]) * LOG2E
        rates = [jnp.broadcast_to(rates[n : n + 1], (requests, LANES)) for n in range(states)]
        start = jnp.swapaxes(state_ref[:, :, lanes].astype(jnp.float32), 0, 1)
        unroll = 4

        def advance(i, held):
            held = list(held)
            for k in range(unroll):
                t = i * unroll + k
                row = pl.ds(pl.multiple_of(t * requests, requests), requests)
                dt = dt_s[row, lanes]
                drive = drive_s[row, lanes]
                sums = [y_s[row, lanes], None, None, None]
                for n in range(states):
                    held[n] = jnp.exp2(dt * rates[n]) * held[n] + drive * bc_s[t, n]
                    term = held[n] * bc_s[t, states + n]
                    q = n % 4
                    sums[q] = term if sums[q] is None else sums[q] + term
                y_s[row, lanes] = (sums[0] + sums[1]) + (sums[2] + sums[3])
            return tuple(held)

        held = lax.fori_loop(
            0, turn // unroll, advance, tuple(start[n] for n in range(states))
        )
        final_ref[:, :, lanes] = jnp.swapaxes(jnp.stack(held), 0, 1)

    span = 16

    def gate(i, _):
        t = pl.multiple_of(i * span, span)
        row = pl.multiple_of(i * span * requests, span * requests)
        y = y_s[pl.ds(row, span * requests), :].reshape(span, requests, width)
        z = z_ref[:, pl.ds(t, span), :].astype(jnp.float32)
        out_ref[:, pl.ds(t, span), :] = (
            jnp.swapaxes(y, 0, 1) * (z / (1.0 + jnp.exp(-z)))
        ).astype(jnp.bfloat16)
        return 0

    lax.fori_loop(0, turn // span, gate, 0)


def scan_gate(
    chunk, turn, norm, conv_out, gate_z, dt_weight, dt_bias, a_log, skip_gain, state, gated
):
    requests, whole, inner = gate_z.shape
    states = a_log.shape[0]
    rank = dt_weight.shape[0]
    cols = norm.shape[1]
    rows = requests * turn
    vector = pl.BlockSpec((1, BLOCK), lambda j: (0, j))
    gate_spec = pl.BlockSpec((requests, turn, BLOCK), lambda j: (0, chunk, j))
    state_spec = pl.BlockSpec((requests, states, BLOCK), lambda j: (0, 0, j))
    in_specs = [
        pl.BlockSpec((rows, cols), lambda j: (0, 0)),
        pl.BlockSpec((rows, BLOCK), lambda j: (0, j)),
        gate_spec,
        pl.BlockSpec((rank, BLOCK), lambda j: (0, j)),
        vector,
        pl.BlockSpec((states, BLOCK), lambda j: (0, j)),
        vector,
        state_spec,
    ]
    args = [
        norm,
        conv_out,
        gate_z,
        dt_weight,
        dt_bias.reshape(1, -1),
        a_log,
        skip_gain.reshape(1, -1),
        state,
    ]
    aliases = {}
    if gated is not None:
        aliases = {len(args): 0}
        in_specs.append(pl.BlockSpec(memory_space=pl.ANY))
        args.append(gated)
    return pl.pallas_call(
        functools.partial(scan_kernel, gated is not None),
        grid=(inner // BLOCK,),
        in_specs=in_specs,
        out_specs=[gate_spec, state_spec],
        out_shape=[
            jax.ShapeDtypeStruct((requests, whole, inner), jnp.bfloat16),
            jax.ShapeDtypeStruct((requests, states, inner), jnp.float32),
        ],
        scratch_shapes=[
            pltpu.VMEM((turn, 2 * states, requests, LANES), jnp.float32),
            pltpu.VMEM((rows, BLOCK), jnp.float32),
            pltpu.VMEM((rows, BLOCK), jnp.float32),
            pltpu.VMEM((rows, BLOCK), jnp.float32),
        ],
        input_output_aliases=aliases,
        compiler_params=pltpu.CompilerParams(vmem_limit_bytes=48 * 1024 * 1024),
        cost_estimate=pl.CostEstimate(
            flops=2 * rows * inner * rank + 6 * rows * inner * states,
            bytes_accessed=rows * inner * 6 + rank * inner * 2,
            transcendentals=rows * inner * states,
        ),
    )(*args)


def body(
    hidden_x,
    gate_z,
    conv_weight,
    conv_bias,
    x_weight,
    dt_weight,
    dt_bias,
    a_log,
    skip_gain,
    ssm_cache,
    conv_cache,
    holder_of,
    slot_of,
):
    groups = lax.axis_size("dp")
    my_index = lax.axis_index("dp")
    requests, whole, _ = hidden_x.shape
    slot_count = ssm_cache.shape[0]
    capacity = slot_count // groups
    state_width = a_log.shape[0]
    rank_width = dt_weight.shape[0]
    kept_rows = conv_cache.shape[1]
    holders = holder_of.reshape(groups, requests)
    places = slot_of.reshape(groups, requests)
    earlier = jnp.arange(requests)[None, :] < jnp.arange(requests)[:, None]
    same_holder = holders[:, :, None] == holders[:, None, :]
    rank_within = jnp.sum((same_holder & earlier[None, :, :]).astype(jnp.int32), axis=2)
    rank_range = jnp.arange(capacity, dtype=jnp.int32)

    paired = groups & (groups - 1) == 0
    order = jnp.arange(groups, dtype=jnp.int32)
    if paired:
        sent_to = my_index ^ order
        came_from = sent_to
        pairs = [[(i, i ^ k) for i in range(groups)] for k in range(groups)]
    else:
        sent_to = (my_index + order) % groups
        came_from = (my_index - order) % groups
        pairs = [[(i, (i + k) % groups) for i in range(groups)] for k in range(groups)]

    def exchange(blocks):
        return [
            block if k == 0 else lax.ppermute(block, "dp", pairs[k])
            for k, block in enumerate(blocks)
        ]

    served = (holders == my_index)[:, None, :] & (
        rank_within[:, None, :] == rank_range[None, :, None]
    )
    occupied = jnp.any(served, axis=2)
    sources = jnp.sum(jnp.where(served, places[:, None, :], 0), axis=2)
    own_holders = holders[my_index]
    own_ranks = rank_within[my_index]
    if paired:
        own_steps = own_holders ^ my_index
    else:
        own_steps = (my_index - own_holders) % groups
    lookup = own_steps * capacity + own_ranks

    wanted = sources[sent_to]
    conv_rows = jnp.swapaxes(conv_cache[wanted.reshape(-1)], 0, 1)
    conv_rows = conv_rows.reshape((kept_rows, groups, capacity) + conv_rows.shape[2:])
    conv_got = exchange([conv_rows[:, k] for k in range(groups)])
    conv_start = jnp.concatenate(conv_got, axis=1)[:, lookup]

    ssm_rows = ssm_cache[wanted].astype(jnp.bfloat16)
    ssm_got = exchange([ssm_rows[k] for k in range(groups)])
    state = jnp.concatenate(ssm_got, axis=0)[lookup]

    own_placed = (own_holders[None, None, :] == sent_to[:, None, None]) & (
        own_ranks[None, None, :] == rank_range[None, :, None]
    )
    picked_rows = jnp.sum(
        jnp.where(own_placed, jnp.arange(requests, dtype=jnp.int32)[None, None, :], 0), axis=2
    )
    targets = jnp.where(occupied, sources, slot_count)[came_from].reshape(-1)

    last_inputs = hidden_x[:, whole - kept_rows :, :][picked_rows]
    last_got = exchange([last_inputs[k] for k in range(groups)])
    new_conv = conv_cache.at[targets].set(
        jnp.concatenate(last_got, axis=0).astype(jnp.float32), mode="drop"
    )

    turn = whole // CHUNKS
    conv_outs, norms = [], []
    for chunk in range(CHUNKS):
        if chunk == 0:
            start = conv_start
        else:
            start = jnp.swapaxes(
                hidden_x[:, chunk * turn - kept_rows : chunk * turn, :], 0, 1
            ).astype(jnp.float32)
        conv_out, projected = conv_project(
            chunk, turn, hidden_x, start, conv_weight, conv_bias, x_weight
        )
        share = lax.psum_scatter(projected, "tensor", scatter_dimension=0, tiled=True)
        norm_share = normalize(share, rank_width, state_width)
        conv_outs.append(conv_out)
        norms.append(lax.all_gather(norm_share, "tensor", axis=0, tiled=True))

    gated = None
    for chunk in range(CHUNKS):
        gated, state = scan_gate(
            chunk,
            turn,
            norms[chunk],
            conv_outs[chunk],
            gate_z,
            dt_weight,
            dt_bias,
            a_log,
            skip_gain,
            state,
            gated,
        )

    final_rows = state[picked_rows].astype(jnp.bfloat16)
    final_got = exchange([final_rows[k] for k in range(groups)])
    new_ssm = ssm_cache.at[targets].set(
        jnp.concatenate(final_got, axis=0).astype(jnp.float32), mode="drop"
    )
    return (gated, new_ssm, new_conv)


def solution(mesh):
    placed = (
        P("dp", None, "tensor"),
        P("dp", None, "tensor"),
        P(None, "tensor"),
        P("tensor"),
        P("tensor", None),
        P(None, "tensor"),
        P("tensor"),
        P(None, "tensor"),
        P("tensor"),
        P("dp", None, "tensor"),
        P("dp", None, "tensor"),
        P(),
        P(),
    )
    return jax.shard_map(
        body,
        mesh=mesh,
        in_specs=placed,
        out_specs=(P("dp", None, "tensor"), P("dp", None, "tensor"), P("dp", None, "tensor")),
        check_vma=False,
    )
```

```python
import functools

import jax
import jax.numpy as jnp
from jax import lax
from jax.experimental import pallas as pl
from jax.experimental.pallas import tpu as pltpu
from jax.sharding import PartitionSpec as P

EPSILON = 1e-06
NORM_FLOOR = 0.25
LOG2E = 1.4426950408889634
CHUNKS = 1
BLOCK = 256
LANES = 128


def silu(value):
    return (0.5 * value) * (1.0 + jnp.tanh(0.5 * value))


def softplus(value):
    small = jnp.exp(-jnp.abs(value))
    series = small * (1.0 - small * (0.5 - small * (1.0 / 3.0 - small * 0.25)))
    return jnp.maximum(value, 0.0) + jnp.where(small < 0.0078125, series, jnp.log(1.0 + small))


def reduce_kernel(
    rank,
    states,
    proj_ref,
    out_ref,
    pair_s,
    send_s,
    recv_s,
    total_s,
    mine_s,
    near_s,
    far_s,
    pair_send,
    pair_recv,
    sum_send,
    sum_recv,
    near_send,
    near_recv,
    far_send,
    far_recv,
):
    chips, share, cols = pair_s.shape
    me = lax.axis_index("tensor")
    core = lax.rem(me, 2)
    chip = lax.div(me, 2)
    partner = chip * 2 + (1 - core)

    def chip_at(offset):
        return lax.rem(chip + offset, chips)

    def block(owner):
        return pl.ds(pl.multiple_of(owner * share, share), share)

    def remote(src, dst, send, recv, target):
        copy = pltpu.make_async_remote_copy(
            src_ref=src,
            dst_ref=dst,
            send_sem=send,
            recv_sem=recv,
            device_id={"tensor": target},
            device_id_type=pl.DeviceIdType.MESH,
        )
        copy.start()
        return copy

    barrier = pltpu.get_barrier_semaphore()
    peers = [partner] + [chip_at(o) * 2 + core for o in range(1, chips)]
    for peer in peers:
        pl.semaphore_signal(
            barrier, inc=1, device_id={"tensor": peer}, device_id_type=pl.DeviceIdType.MESH
        )
    pl.semaphore_wait(barrier, chips)

    pairs, sums, nears, fars = {}, {}, {}, {}
    for o in list(range(1, chips)) + [0]:
        owner = chip_at(o) * 2 + (1 - core)
        pairs[o] = remote(
            proj_ref.at[block(owner)], pair_s.at[o], pair_send.at[o], pair_recv.at[o], partner
        )
    for o in range(1, chips):
        owner = chip_at(o) * 2 + core
        pairs[o].wait_recv()
        send_s[o] = (proj_ref[block(owner), :] + pair_s[o]).astype(jnp.bfloat16)
        sums[o] = remote(send_s.at[o], recv_s.at[o], sum_send.at[o], sum_recv.at[o], owner)
    pairs[0].wait_recv()
    total_s[...] = proj_ref[block(me), :] + pair_s[0]
    for o in range(1, chips):
        sums[o].wait_recv()
        total_s[...] += recv_s[o].astype(jnp.float32)

    head = total_s[:, :rank]
    mean = jnp.sum(head * head, axis=1, keepdims=True) / rank
    mine_s[:, :rank] = (head * lax.rsqrt(mean + EPSILON)).astype(jnp.bfloat16)
    tail = total_s[:, rank:]
    square = tail * tail
    inject = lax.broadcasted_iota(jnp.int32, tail.shape, 1) < states
    first = jnp.sum(jnp.where(inject, square, 0.0), axis=1, keepdims=True) / states
    second = jnp.sum(jnp.where(inject, 0.0, square), axis=1, keepdims=True) / states
    scale = jnp.where(
        inject,
        lax.rsqrt(jnp.maximum(first, NORM_FLOOR)),
        lax.rsqrt(jnp.maximum(second, NORM_FLOOR)),
    )
    mine_s[:, rank:] = (tail * scale).astype(jnp.bfloat16)

    for o in range(1, chips):
        nears[o] = remote(
            mine_s, near_s.at[o], near_send.at[o], near_recv.at[o], chip_at(o) * 2 + core
        )
    fars[0] = remote(mine_s, far_s.at[0], far_send.at[0], far_recv.at[0], partner)
    out_ref[block(me), :] = mine_s[...]
    for o in range(1, chips):
        nears[o].wait_recv()
        fars[o] = remote(near_s.at[o], far_s.at[o], far_send.at[o], far_recv.at[o], partner)
        out_ref[block(chip_at(chips - o) * 2 + core), :] = near_s[o]
    for o in range(chips):
        fars[o].wait_recv()
        out_ref[block(chip_at(chips - o) * 2 + (1 - core)), :] = far_s[o]
    for group in (pairs, sums, nears, fars):
        for copy in group.values():
            copy.wait_send()


def reduce_norm(projected, rank, states):
    rows, cols = projected.shape
    devices = lax.axis_size("tensor")
    chips = devices // 2
    share = rows // devices
    shape = (chips, share, cols)
    return pl.pallas_call(
        functools.partial(reduce_kernel, rank, states),
        in_specs=[pl.BlockSpec(memory_space=pltpu.VMEM)],
        out_specs=pl.BlockSpec(memory_space=pltpu.VMEM),
        out_shape=jax.ShapeDtypeStruct((rows, cols), jnp.bfloat16),
        scratch_shapes=[
            pltpu.VMEM(shape, jnp.float32),
            pltpu.VMEM(shape, jnp.bfloat16),
            pltpu.VMEM(shape, jnp.bfloat16),
            pltpu.VMEM(shape[1:], jnp.float32),
            pltpu.VMEM(shape[1:], jnp.bfloat16),
            pltpu.VMEM(shape, jnp.bfloat16),
            pltpu.VMEM(shape, jnp.bfloat16),
        ]
        + [pltpu.SemaphoreType.DMA((chips,))] * 8,
        compiler_params=pltpu.CompilerParams(
            collective_id=1, has_side_effects=True, vmem_limit_bytes=24 * 1024 * 1024
        ),
        cost_estimate=pl.CostEstimate(
            flops=rows * cols * 4, bytes_accessed=40000000, transcendentals=0
        ),
    )(projected)


def conv_kernel(x_ref, start_ref, cw_ref, cb_ref, xw_ref, out_ref, proj_ref, ext):
    step = pl.program_id(0)
    requests, turn, width = x_ref.shape
    taps = cw_ref.shape[0]
    tile = 16
    ext[0 : taps - 1] = start_ref[...]

    def gather(i, _):
        t = pl.multiple_of(i * tile, tile)
        rows = x_ref[:, pl.ds(t, tile), :].astype(jnp.float32)
        ext[pl.ds(taps - 1 + t, tile)] = jnp.swapaxes(rows, 0, 1)
        return 0

    lax.fori_loop(0, turn // tile, gather, 0)
    weights = [cw_ref[j : j + 1, :][None] for j in range(taps)]
    bias = cb_ref[...][None]

    def convolve(i, _):
        t = i * tile
        total = ext[pl.ds(t, tile)] * weights[0] + bias
        for j in range(1, taps):
            total = total + ext[pl.ds(t + j, tile)] * weights[j]
        value = silu(total)
        row = pl.multiple_of(t * requests, tile * requests)
        out_ref[pl.ds(row, tile * requests), :] = value.reshape(tile * requests, width).astype(
            jnp.bfloat16
        )
        return 0

    lax.fori_loop(0, turn // tile, convolve, 0)

    @pl.when(step == 0)
    def _():
        proj_ref[...] = jnp.dot(out_ref[...], xw_ref[...], preferred_element_type=jnp.float32)

    @pl.when(step > 0)
    def _():
        proj_ref[...] += jnp.dot(out_ref[...], xw_ref[...], preferred_element_type=jnp.float32)


def conv_project(chunk, turn, hidden_x, start, conv_weight, conv_bias, x_weight):
    requests, _, inner = hidden_x.shape
    taps = conv_weight.shape[0]
    cols = x_weight.shape[1]
    rows = requests * turn
    return pl.pallas_call(
        conv_kernel,
        grid=(inner // BLOCK,),
        in_specs=[
            pl.BlockSpec((requests, turn, BLOCK), lambda j: (0, chunk, j)),
            pl.BlockSpec((taps - 1, requests, BLOCK), lambda j: (0, 0, j)),
            pl.BlockSpec((taps, BLOCK), lambda j: (0, j)),
            pl.BlockSpec((1, BLOCK), lambda j: (0, j)),
            pl.BlockSpec((BLOCK, cols), lambda j: (j, 0)),
        ],
        out_specs=[
            pl.BlockSpec((rows, BLOCK), lambda j: (0, j)),
            pl.BlockSpec((rows, cols), lambda j: (0, 0)),
        ],
        out_shape=[
            jax.ShapeDtypeStruct((rows, inner), jnp.bfloat16),
            jax.ShapeDtypeStruct((rows, cols), jnp.float32),
        ],
        scratch_shapes=[pltpu.VMEM((turn + taps - 1, requests, BLOCK), jnp.float32)],
        compiler_params=pltpu.CompilerParams(vmem_limit_bytes=40 * 1024 * 1024),
        cost_estimate=pl.CostEstimate(
            flops=2 * rows * inner * cols,
            bytes_accessed=rows * inner * 4 + inner * cols * 2 + rows * cols * 4,
            transcendentals=2 * rows * inner,
        ),
    )(hidden_x, start, conv_weight, conv_bias.reshape(1, -1), x_weight)


def scan_kernel(
    aliased,
    norm_ref,
    x_ref,
    z_ref,
    dtw_ref,
    dtb_ref,
    alog_ref,
    skip_ref,
    state_ref,
    *rest,
):
    if aliased:
        rest = rest[1:]
    out_ref, final_ref, bc_s, dt_s, drive_s, y_s = rest
    step = pl.program_id(0)
    requests, turn, width = z_ref.shape
    states = alog_ref.shape[0]
    rank = dtw_ref.shape[0]
    rows = requests * turn
    tile = 128

    @pl.when(step == 0)
    def _():
        def spread(i, _):
            row = pl.multiple_of(i * 16, 16)
            both = norm_ref[pl.ds(row, 16), rank:].astype(jnp.float32)
            for half in range(16 // requests):
                part = both[half * requests : (half + 1) * requests]
                t = i * (16 // requests) + half
                for n in range(2 * states):
                    bc_s[t, n] = jnp.broadcast_to(part[:, n : n + 1], (requests, LANES))
            return 0

        lax.fori_loop(0, rows // 16, spread, 0)

    bias = dtb_ref[...]
    skip = skip_ref[...]

    def steps(i, _):
        row = pl.multiple_of(i * tile, tile)
        raw = jnp.dot(
            norm_ref[pl.ds(row, tile), :rank], dtw_ref[...], preferred_element_type=jnp.float32
        )
        raw = raw + bias
        dt = softplus(raw)
        x = x_ref[pl.ds(row, tile), :].astype(jnp.float32)
        dt_s[pl.ds(row, tile), :] = dt
        drive_s[pl.ds(row, tile), :] = dt * x
        y_s[pl.ds(row, tile), :] = skip * x
        return 0

    lax.fori_loop(0, rows // tile, steps, 0)

    for part in range(width // LANES):
        lanes = slice(part * LANES, (part + 1) * LANES)
        rates = -jnp.exp(alog_ref[:, lanes]) * LOG2E
        rates = [jnp.broadcast_to(rates[n : n + 1], (requests, LANES)) for n in range(states)]
        start = jnp.swapaxes(state_ref[:, :, lanes].astype(jnp.float32), 0, 1)
        unroll = 8

        def advance(i, held):
            held = list(held)
            for k in range(unroll):
                t = i * unroll + k
                row = pl.ds(pl.multiple_of(t * requests, requests), requests)
                dt = dt_s[row, lanes]
                drive = drive_s[row, lanes]
                sums = [y_s[row, lanes], None, None, None]
                for n in range(states):
                    held[n] = jnp.exp2(dt * rates[n]) * held[n] + drive * bc_s[t, n]
                    term = held[n] * bc_s[t, states + n]
                    q = n % 4
                    sums[q] = term if sums[q] is None else sums[q] + term
                y_s[row, lanes] = (sums[0] + sums[1]) + (sums[2] + sums[3])
            return tuple(held)

        held = lax.fori_loop(
            0, turn // unroll, advance, tuple(start[n] for n in range(states))
        )
        final_ref[:, :, lanes] = jnp.swapaxes(jnp.stack(held), 0, 1)

    span = 16

    def gate(i, _):
        t = pl.multiple_of(i * span, span)
        row = pl.multiple_of(i * span * requests, span * requests)
        y = y_s[pl.ds(row, span * requests), :].reshape(span, requests, width)
        z = z_ref[:, pl.ds(t, span), :].astype(jnp.float32)
        out_ref[:, pl.ds(t, span), :] = (
            jnp.swapaxes(y, 0, 1) * silu(z)
        ).astype(jnp.bfloat16)
        return 0

    lax.fori_loop(0, turn // span, gate, 0)


def scan_gate(
    chunk, turn, norm, conv_out, gate_z, dt_weight, dt_bias, a_log, skip_gain, state, gated
):
    requests, whole, inner = gate_z.shape
    states = a_log.shape[0]
    rank = dt_weight.shape[0]
    cols = norm.shape[1]
    rows = requests * turn
    vector = pl.BlockSpec((1, BLOCK), lambda j: (0, j))
    gate_spec = pl.BlockSpec((requests, turn, BLOCK), lambda j: (0, chunk, j))
    state_spec = pl.BlockSpec((requests, states, BLOCK), lambda j: (0, 0, j))
    in_specs = [
        pl.BlockSpec((rows, cols), lambda j: (0, 0)),
        pl.BlockSpec((rows, BLOCK), lambda j: (0, j)),
        gate_spec,
        pl.BlockSpec((rank, BLOCK), lambda j: (0, j)),
        vector,
        pl.BlockSpec((states, BLOCK), lambda j: (0, j)),
        vector,
        state_spec,
    ]
    args = [
        norm,
        conv_out,
        gate_z,
        dt_weight,
        dt_bias.reshape(1, -1),
        a_log,
        skip_gain.reshape(1, -1),
        state,
    ]
    aliases = {}
    if gated is not None:
        aliases = {len(args): 0}
        in_specs.append(pl.BlockSpec(memory_space=pl.ANY))
        args.append(gated)
    return pl.pallas_call(
        functools.partial(scan_kernel, gated is not None),
        grid=(inner // BLOCK,),
        in_specs=in_specs,
        out_specs=[gate_spec, state_spec],
        out_shape=[
            jax.ShapeDtypeStruct((requests, whole, inner), jnp.bfloat16),
            jax.ShapeDtypeStruct((requests, states, inner), jnp.float32),
        ],
        scratch_shapes=[
            pltpu.VMEM((turn, 2 * states, requests, LANES), jnp.float32),
            pltpu.VMEM((rows, BLOCK), jnp.float32),
            pltpu.VMEM((rows, BLOCK), jnp.float32),
            pltpu.VMEM((rows, BLOCK), jnp.float32),
        ],
        input_output_aliases=aliases,
        compiler_params=pltpu.CompilerParams(vmem_limit_bytes=48 * 1024 * 1024),
        cost_estimate=pl.CostEstimate(
            flops=2 * rows * inner * rank + 6 * rows * inner * states,
            bytes_accessed=rows * inner * 6 + rank * inner * 2,
            transcendentals=rows * inner * states,
        ),
    )(*args)


def body(
    hidden_x,
    gate_z,
    conv_weight,
    conv_bias,
    x_weight,
    dt_weight,
    dt_bias,
    a_log,
    skip_gain,
    ssm_cache,
    conv_cache,
    holder_of,
    slot_of,
):
    groups = lax.axis_size("dp")
    my_index = lax.axis_index("dp")
    requests, whole, _ = hidden_x.shape
    slot_count = ssm_cache.shape[0]
    capacity = slot_count // groups
    state_width = a_log.shape[0]
    rank_width = dt_weight.shape[0]
    kept_rows = conv_cache.shape[1]
    holders = holder_of.reshape(groups, requests)
    places = slot_of.reshape(groups, requests)
    earlier = jnp.arange(requests)[None, :] < jnp.arange(requests)[:, None]
    same_holder = holders[:, :, None] == holders[:, None, :]
    rank_within = jnp.sum((same_holder & earlier[None, :, :]).astype(jnp.int32), axis=2)
    rank_range = jnp.arange(capacity, dtype=jnp.int32)

    paired = groups & (groups - 1) == 0
    order = jnp.arange(groups, dtype=jnp.int32)
    if paired:
        sent_to = my_index ^ order
        came_from = sent_to
        pairs = [[(i, i ^ k) for i in range(groups)] for k in range(groups)]
    else:
        sent_to = (my_index + order) % groups
        came_from = (my_index - order) % groups
        pairs = [[(i, (i + k) % groups) for i in range(groups)] for k in range(groups)]

    def exchange(blocks):
        return [
            block if k == 0 else lax.ppermute(block, "dp", pairs[k])
            for k, block in enumerate(blocks)
        ]

    served = (holders == my_index)[:, None, :] & (
        rank_within[:, None, :] == rank_range[None, :, None]
    )
    occupied = jnp.any(served, axis=2)
    sources = jnp.sum(jnp.where(served, places[:, None, :], 0), axis=2)
    own_holders = holders[my_index]
    own_ranks = rank_within[my_index]
    if paired:
        own_steps = own_holders ^ my_index
    else:
        own_steps = (my_index - own_holders) % groups
    lookup = own_steps * capacity + own_ranks

    wanted = sources[sent_to]
    conv_rows = jnp.swapaxes(conv_cache[wanted.reshape(-1)], 0, 1)
    conv_rows = conv_rows.reshape((kept_rows, groups, capacity) + conv_rows.shape[2:])
    conv_got = exchange([conv_rows[:, k] for k in range(groups)])
    conv_start = jnp.concatenate(conv_got, axis=1)[:, lookup]

    ssm_rows = ssm_cache[wanted].astype(jnp.bfloat16)
    ssm_got = exchange([ssm_rows[k] for k in range(groups)])
    state = jnp.concatenate(ssm_got, axis=0)[lookup]

    own_placed = (own_holders[None, None, :] == sent_to[:, None, None]) & (
        own_ranks[None, None, :] == rank_range[None, :, None]
    )
    picked_rows = jnp.sum(
        jnp.where(own_placed, jnp.arange(requests, dtype=jnp.int32)[None, None, :], 0), axis=2
    )
    targets = jnp.where(occupied, sources, slot_count)[came_from].reshape(-1)

    last_inputs = hidden_x[:, whole - kept_rows :, :][picked_rows]
    last_got = exchange([last_inputs[k] for k in range(groups)])
    new_conv = conv_cache.at[targets].set(
        jnp.concatenate(last_got, axis=0).astype(jnp.float32), mode="drop"
    )

    turn = whole // CHUNKS
    conv_outs, norms = [], []
    for chunk in range(CHUNKS):
        if chunk == 0:
            start = conv_start
        else:
            start = jnp.swapaxes(
                hidden_x[:, chunk * turn - kept_rows : chunk * turn, :], 0, 1
            ).astype(jnp.float32)
        conv_out, projected = conv_project(
            chunk, turn, hidden_x, start, conv_weight, conv_bias, x_weight
        )
        conv_outs.append(conv_out)
        norms.append(reduce_norm(projected, rank_width, state_width))

    gated = None
    for chunk in range(CHUNKS):
        gated, state = scan_gate(
            chunk,
            turn,
            norms[chunk],
            conv_outs[chunk],
            gate_z,
            dt_weight,
            dt_bias,
            a_log,
            skip_gain,
            state,
            gated,
        )

    final_rows = state[picked_rows].astype(jnp.bfloat16)
    final_got = exchange([final_rows[k] for k in range(groups)])
    new_ssm = ssm_cache.at[targets].set(
        jnp.concatenate(final_got, axis=0).astype(jnp.float32), mode="drop"
    )
    return (gated, new_ssm, new_conv)


def solution(mesh):
    placed = (
        P("dp", None, "tensor"),
        P("dp", None, "tensor"),
        P(None, "tensor"),
        P("tensor"),
        P("tensor", None),
        P(None, "tensor"),
        P("tensor"),
        P(None, "tensor"),
        P("tensor"),
        P("dp", None, "tensor"),
        P("dp", None, "tensor"),
        P(),
        P(),
    )
    return jax.shard_map(
        body,
        mesh=mesh,
        in_specs=placed,
        out_specs=(P("dp", None, "tensor"), P("dp", None, "tensor"), P("dp", None, "tensor")),
        check_vma=False,
    )
```

```python
import functools

import jax
import jax.numpy as jnp
from jax import lax
from jax.experimental import pallas as pl
from jax.experimental.pallas import tpu as pltpu
from jax.sharding import PartitionSpec as P

EPSILON = 1e-06
NORM_FLOOR = 0.25
CHUNKS = 1
BLOCK = 256
LANES = 128


def silu(value):
    return (0.5 * value) * (1.0 + jnp.tanh(0.5 * value))


def softplus(value):
    small = jnp.exp(-jnp.abs(value))
    series = small * (1.0 - small * (0.5 - small * (1.0 / 3.0 - small * 0.25)))
    return jnp.maximum(value, 0.0) + jnp.where(small < 0.0078125, series, jnp.log(1.0 + small))


def reduce_kernel(
    rank,
    states,
    proj_ref,
    out_ref,
    pair_s,
    send_s,
    recv_s,
    total_s,
    mine_s,
    near_s,
    far_s,
    pair_send,
    pair_recv,
    sum_send,
    sum_recv,
    near_send,
    near_recv,
    far_send,
    far_recv,
):
    chips, share, cols = pair_s.shape
    me = lax.axis_index("tensor")
    core = lax.rem(me, 2)
    chip = lax.div(me, 2)
    partner = chip * 2 + (1 - core)

    def chip_at(offset):
        return lax.rem(chip + offset, chips)

    def block(owner):
        return pl.ds(pl.multiple_of(owner * share, share), share)

    def remote(src, dst, send, recv, target):
        copy = pltpu.make_async_remote_copy(
            src_ref=src,
            dst_ref=dst,
            send_sem=send,
            recv_sem=recv,
            device_id={"tensor": target},
            device_id_type=pl.DeviceIdType.MESH,
        )
        copy.start()
        return copy

    barrier = pltpu.get_barrier_semaphore()
    peers = [partner] + [chip_at(o) * 2 + core for o in range(1, chips)]
    for peer in peers:
        pl.semaphore_signal(
            barrier, inc=1, device_id={"tensor": peer}, device_id_type=pl.DeviceIdType.MESH
        )
    pl.semaphore_wait(barrier, chips)

    pairs, sums, nears, fars = {}, {}, {}, {}
    for o in list(range(1, chips)) + [0]:
        owner = chip_at(o) * 2 + (1 - core)
        pairs[o] = remote(
            proj_ref.at[block(owner)], pair_s.at[o], pair_send.at[o], pair_recv.at[o], partner
        )
    for o in range(1, chips):
        owner = chip_at(o) * 2 + core
        pairs[o].wait_recv()
        send_s[o] = (proj_ref[block(owner), :] + pair_s[o]).astype(jnp.bfloat16)
        sums[o] = remote(send_s.at[o], recv_s.at[o], sum_send.at[o], sum_recv.at[o], owner)
    pairs[0].wait_recv()
    total_s[...] = proj_ref[block(me), :] + pair_s[0]
    for o in range(1, chips):
        sums[o].wait_recv()
        total_s[...] += recv_s[o].astype(jnp.float32)

    head = total_s[:, :rank]
    mean = jnp.sum(head * head, axis=1, keepdims=True) / rank
    mine_s[:, :rank] = (head * lax.rsqrt(mean + EPSILON)).astype(jnp.bfloat16)
    tail = total_s[:, rank:]
    square = tail * tail
    inject = lax.broadcasted_iota(jnp.int32, tail.shape, 1) < states
    first = jnp.sum(jnp.where(inject, square, 0.0), axis=1, keepdims=True) / states
    second = jnp.sum(jnp.where(inject, 0.0, square), axis=1, keepdims=True) / states
    scale = jnp.where(
        inject,
        lax.rsqrt(jnp.maximum(first, NORM_FLOOR)),
        lax.rsqrt(jnp.maximum(second, NORM_FLOOR)),
    )
    mine_s[:, rank:] = (tail * scale).astype(jnp.bfloat16)

    for o in range(1, chips):
        nears[o] = remote(
            mine_s, near_s.at[o], near_send.at[o], near_recv.at[o], chip_at(o) * 2 + core
        )
    fars[0] = remote(mine_s, far_s.at[0], far_send.at[0], far_recv.at[0], partner)
    out_ref[block(me), :] = mine_s[...]
    for o in range(1, chips):
        nears[o].wait_recv()
        fars[o] = remote(near_s.at[o], far_s.at[o], far_send.at[o], far_recv.at[o], partner)
        out_ref[block(chip_at(chips - o) * 2 + core), :] = near_s[o]
    for o in range(chips):
        fars[o].wait_recv()
        out_ref[block(chip_at(chips - o) * 2 + (1 - core)), :] = far_s[o]
    for group in (pairs, sums, nears, fars):
        for copy in group.values():
            copy.wait_send()


def reduce_norm(projected, rank, states):
    rows, cols = projected.shape
    devices = lax.axis_size("tensor")
    chips = devices // 2
    share = rows // devices
    shape = (chips, share, cols)
    return pl.pallas_call(
        functools.partial(reduce_kernel, rank, states),
        in_specs=[pl.BlockSpec(memory_space=pltpu.VMEM)],
        out_specs=pl.BlockSpec(memory_space=pltpu.VMEM),
        out_shape=jax.ShapeDtypeStruct((rows, cols), jnp.bfloat16),
        scratch_shapes=[
            pltpu.VMEM(shape, jnp.float32),
            pltpu.VMEM(shape, jnp.bfloat16),
            pltpu.VMEM(shape, jnp.bfloat16),
            pltpu.VMEM(shape[1:], jnp.float32),
            pltpu.VMEM(shape[1:], jnp.bfloat16),
            pltpu.VMEM(shape, jnp.bfloat16),
            pltpu.VMEM(shape, jnp.bfloat16),
        ]
        + [pltpu.SemaphoreType.DMA((chips,))] * 8,
        compiler_params=pltpu.CompilerParams(
            collective_id=1, has_side_effects=True, vmem_limit_bytes=24 * 1024 * 1024
        ),
        cost_estimate=pl.CostEstimate(
            flops=rows * cols * 4, bytes_accessed=40000000, transcendentals=0
        ),
    )(projected)


def conv_kernel(x_ref, start_ref, cw_ref, cb_ref, xw_ref, out_ref, proj_ref, ext):
    step = pl.program_id(0)
    requests, turn, width = x_ref.shape
    taps = cw_ref.shape[0]
    tile = 16
    ext[0 : taps - 1] = start_ref[...]

    def gather(i, _):
        t = pl.multiple_of(i * tile, tile)
        rows = x_ref[:, pl.ds(t, tile), :].astype(jnp.float32)
        ext[pl.ds(taps - 1 + t, tile)] = jnp.swapaxes(rows, 0, 1)
        return 0

    lax.fori_loop(0, turn // tile, gather, 0)
    weights = [cw_ref[j : j + 1, :][None] for j in range(taps)]
    bias = cb_ref[...][None]

    def convolve(i, _):
        t = i * tile
        total = ext[pl.ds(t, tile)] * weights[0] + bias
        for j in range(1, taps):
            total = total + ext[pl.ds(t + j, tile)] * weights[j]
        value = silu(total)
        row = pl.multiple_of(t * requests, tile * requests)
        out_ref[pl.ds(row, tile * requests), :] = value.reshape(tile * requests, width).astype(
            jnp.bfloat16
        )
        return 0

    lax.fori_loop(0, turn // tile, convolve, 0)

    @pl.when(step == 0)
    def _():
        proj_ref[...] = jnp.dot(out_ref[...], xw_ref[...], preferred_element_type=jnp.float32)

    @pl.when(step > 0)
    def _():
        proj_ref[...] += jnp.dot(out_ref[...], xw_ref[...], preferred_element_type=jnp.float32)


def conv_project(chunk, turn, hidden_x, start, conv_weight, conv_bias, x_weight):
    requests, _, inner = hidden_x.shape
    taps = conv_weight.shape[0]
    cols = x_weight.shape[1]
    rows = requests * turn
    return pl.pallas_call(
        conv_kernel,
        grid=(inner // BLOCK,),
        in_specs=[
            pl.BlockSpec((requests, turn, BLOCK), lambda j: (0, chunk, j)),
            pl.BlockSpec((taps - 1, requests, BLOCK), lambda j: (0, 0, j)),
            pl.BlockSpec((taps, BLOCK), lambda j: (0, j)),
            pl.BlockSpec((1, BLOCK), lambda j: (0, j)),
            pl.BlockSpec((BLOCK, cols), lambda j: (j, 0)),
        ],
        out_specs=[
            pl.BlockSpec((rows, BLOCK), lambda j: (0, j)),
            pl.BlockSpec((rows, cols), lambda j: (0, 0)),
        ],
        out_shape=[
            jax.ShapeDtypeStruct((rows, inner), jnp.bfloat16),
            jax.ShapeDtypeStruct((rows, cols), jnp.float32),
        ],
        scratch_shapes=[pltpu.VMEM((turn + taps - 1, requests, BLOCK), jnp.float32)],
        compiler_params=pltpu.CompilerParams(vmem_limit_bytes=40 * 1024 * 1024),
        cost_estimate=pl.CostEstimate(
            flops=2 * rows * inner * cols,
            bytes_accessed=rows * inner * 4 + inner * cols * 2 + rows * cols * 4,
            transcendentals=2 * rows * inner,
        ),
    )(hidden_x, start, conv_weight, conv_bias.reshape(1, -1), x_weight)


def scan_kernel(
    aliased,
    norm_ref,
    x_ref,
    z_ref,
    dtw_ref,
    dtb_ref,
    alog_ref,
    skip_ref,
    state_ref,
    *rest,
):
    if aliased:
        rest = rest[1:]
    out_ref, final_ref, bc_s, dt_s, drive_s, y_s = rest
    step = pl.program_id(0)
    requests, turn, width = z_ref.shape
    states = alog_ref.shape[0]
    rank = dtw_ref.shape[0]
    rows = requests * turn
    tile = 128

    @pl.when(step == 0)
    def _():
        def spread(i, _):
            row = pl.multiple_of(i * 16, 16)
            both = norm_ref[pl.ds(row, 16), rank:].astype(jnp.float32)
            for half in range(16 // requests):
                part = both[half * requests : (half + 1) * requests]
                t = i * (16 // requests) + half
                for n in range(2 * states):
                    bc_s[t, n] = jnp.broadcast_to(part[:, n : n + 1], (requests, LANES))
            return 0

        lax.fori_loop(0, rows // 16, spread, 0)

    bias = dtb_ref[...]
    skip = skip_ref[...]

    def steps(i, _):
        row = pl.multiple_of(i * tile, tile)
        raw = jnp.dot(
            norm_ref[pl.ds(row, tile), :rank], dtw_ref[...], preferred_element_type=jnp.float32
        )
        raw = raw + bias
        dt = softplus(raw)
        x = x_ref[pl.ds(row, tile), :].astype(jnp.float32)
        dt_s[pl.ds(row, tile), :] = dt
        drive_s[pl.ds(row, tile), :] = dt * x
        y_s[pl.ds(row, tile), :] = skip * x
        return 0

    lax.fori_loop(0, rows // tile, steps, 0)

    for part in range(width // LANES):
        lanes = slice(part * LANES, (part + 1) * LANES)
        rates = -jnp.exp(alog_ref[:, lanes])
        rates = [jnp.broadcast_to(rates[n : n + 1], (requests, LANES)) for n in range(states)]
        start = jnp.swapaxes(state_ref[:, :, lanes].astype(jnp.float32), 0, 1)
        unroll = 8

        def advance(i, held):
            held = list(held)
            for k in range(unroll):
                t = i * unroll + k
                row = pl.ds(pl.multiple_of(t * requests, requests), requests)
                dt = dt_s[row, lanes]
                drive = drive_s[row, lanes]
                sums = [y_s[row, lanes], None, None, None]
                for n in range(states):
                    held[n] = jnp.exp(dt * rates[n]) * held[n] + drive * bc_s[t, n]
                    term = held[n] * bc_s[t, states + n]
                    q = n % 4
                    sums[q] = term if sums[q] is None else sums[q] + term
                y_s[row, lanes] = (sums[0] + sums[1]) + (sums[2] + sums[3])
            return tuple(held)

        held = lax.fori_loop(
            0, turn // unroll, advance, tuple(start[n] for n in range(states))
        )
        final_ref[:, :, lanes] = jnp.swapaxes(jnp.stack(held), 0, 1)

    span = 16

    def gate(i, _):
        t = pl.multiple_of(i * span, span)
        row = pl.multiple_of(i * span * requests, span * requests)
        y = y_s[pl.ds(row, span * requests), :].reshape(span, requests, width)
        z = z_ref[:, pl.ds(t, span), :].astype(jnp.float32)
        out_ref[:, pl.ds(t, span), :] = (
            jnp.swapaxes(y, 0, 1) * silu(z)
        ).astype(jnp.bfloat16)
        return 0

    lax.fori_loop(0, turn // span, gate, 0)


def scan_gate(
    chunk, turn, norm, conv_out, gate_z, dt_weight, dt_bias, a_log, skip_gain, state, gated
):
    requests, whole, inner = gate_z.shape
    states = a_log.shape[0]
    rank = dt_weight.shape[0]
    cols = norm.shape[1]
    rows = requests * turn
    vector = pl.BlockSpec((1, BLOCK), lambda j: (0, j))
    gate_spec = pl.BlockSpec((requests, turn, BLOCK), lambda j: (0, chunk, j))
    state_spec = pl.BlockSpec((requests, states, BLOCK), lambda j: (0, 0, j))
    in_specs = [
        pl.BlockSpec((rows, cols), lambda j: (0, 0)),
        pl.BlockSpec((rows, BLOCK), lambda j: (0, j)),
        gate_spec,
        pl.BlockSpec((rank, BLOCK), lambda j: (0, j)),
        vector,
        pl.BlockSpec((states, BLOCK), lambda j: (0, j)),
        vector,
        state_spec,
    ]
    args = [
        norm,
        conv_out,
        gate_z,
        dt_weight,
        dt_bias.reshape(1, -1),
        a_log,
        skip_gain.reshape(1, -1),
        state,
    ]
    aliases = {}
    if gated is not None:
        aliases = {len(args): 0}
        in_specs.append(pl.BlockSpec(memory_space=pl.ANY))
        args.append(gated)
    return pl.pallas_call(
        functools.partial(scan_kernel, gated is not None),
        grid=(inner // BLOCK,),
        in_specs=in_specs,
        out_specs=[gate_spec, state_spec],
        out_shape=[
            jax.ShapeDtypeStruct((requests, whole, inner), jnp.bfloat16),
            jax.ShapeDtypeStruct((requests, states, inner), jnp.float32),
        ],
        scratch_shapes=[
            pltpu.VMEM((turn, 2 * states, requests, LANES), jnp.float32),
            pltpu.VMEM((rows, BLOCK), jnp.float32),
            pltpu.VMEM((rows, BLOCK), jnp.float32),
            pltpu.VMEM((rows, BLOCK), jnp.float32),
        ],
        input_output_aliases=aliases,
        compiler_params=pltpu.CompilerParams(vmem_limit_bytes=48 * 1024 * 1024),
        cost_estimate=pl.CostEstimate(
            flops=2 * rows * inner * rank + 6 * rows * inner * states,
            bytes_accessed=rows * inner * 6 + rank * inner * 2,
            transcendentals=rows * inner * states,
        ),
    )(*args)


def body(
    hidden_x,
    gate_z,
    conv_weight,
    conv_bias,
    x_weight,
    dt_weight,
    dt_bias,
    a_log,
    skip_gain,
    ssm_cache,
    conv_cache,
    holder_of,
    slot_of,
):
    groups = lax.axis_size("dp")
    my_index = lax.axis_index("dp")
    requests, whole, _ = hidden_x.shape
    slot_count = ssm_cache.shape[0]
    capacity = slot_count // groups
    state_width = a_log.shape[0]
    rank_width = dt_weight.shape[0]
    kept_rows = conv_cache.shape[1]
    holders = holder_of.reshape(groups, requests)
    places = slot_of.reshape(groups, requests)
    earlier = jnp.arange(requests)[None, :] < jnp.arange(requests)[:, None]
    same_holder = holders[:, :, None] == holders[:, None, :]
    rank_within = jnp.sum((same_holder & earlier[None, :, :]).astype(jnp.int32), axis=2)
    rank_range = jnp.arange(capacity, dtype=jnp.int32)

    paired = groups & (groups - 1) == 0
    order = jnp.arange(groups, dtype=jnp.int32)
    if paired:
        sent_to = my_index ^ order
        came_from = sent_to
        pairs = [[(i, i ^ k) for i in range(groups)] for k in range(groups)]
    else:
        sent_to = (my_index + order) % groups
        came_from = (my_index - order) % groups
        pairs = [[(i, (i + k) % groups) for i in range(groups)] for k in range(groups)]

    def exchange(blocks):
        return [
            block if k == 0 else lax.ppermute(block, "dp", pairs[k])
            for k, block in enumerate(blocks)
        ]

    served = (holders == my_index)[:, None, :] & (
        rank_within[:, None, :] == rank_range[None, :, None]
    )
    occupied = jnp.any(served, axis=2)
    sources = jnp.sum(jnp.where(served, places[:, None, :], 0), axis=2)
    own_holders = holders[my_index]
    own_ranks = rank_within[my_index]
    if paired:
        own_steps = own_holders ^ my_index
    else:
        own_steps = (my_index - own_holders) % groups
    lookup = own_steps * capacity + own_ranks

    wanted = sources[sent_to]
    conv_rows = jnp.swapaxes(conv_cache[wanted.reshape(-1)], 0, 1)
    conv_rows = conv_rows.reshape((kept_rows, groups, capacity) + conv_rows.shape[2:])
    conv_got = exchange([conv_rows[:, k] for k in range(groups)])
    conv_start = jnp.concatenate(conv_got, axis=1)[:, lookup]

    turn = whole // CHUNKS
    conv_outs, products = [], []
    for chunk in range(CHUNKS):
        if chunk == 0:
            start = conv_start
        else:
            start = jnp.swapaxes(
                hidden_x[:, chunk * turn - kept_rows : chunk * turn, :], 0, 1
            ).astype(jnp.float32)
        conv_out, projected = conv_project(
            chunk, turn, hidden_x, start, conv_weight, conv_bias, x_weight
        )
        conv_outs.append(conv_out)
        products.append(projected)

    wanted_late, targets_late, products[0] = lax.optimization_barrier(
        (wanted, sent_to, products[0])
    )
    ssm_rows = ssm_cache[wanted_late].astype(jnp.bfloat16)
    ssm_got = exchange([ssm_rows[k] for k in range(groups)])
    state = jnp.concatenate(ssm_got, axis=0)[lookup]

    own_placed = (own_holders[None, None, :] == targets_late[:, None, None]) & (
        own_ranks[None, None, :] == rank_range[None, :, None]
    )
    picked_rows = jnp.sum(
        jnp.where(own_placed, jnp.arange(requests, dtype=jnp.int32)[None, None, :], 0), axis=2
    )
    targets = jnp.where(occupied, sources, slot_count)[came_from].reshape(-1)

    last_inputs = hidden_x[:, whole - kept_rows :, :][picked_rows]
    last_got = exchange([last_inputs[k] for k in range(groups)])
    new_conv = conv_cache.at[targets].set(
        jnp.concatenate(last_got, axis=0).astype(jnp.float32), mode="drop"
    )

    norms = [reduce_norm(product, rank_width, state_width) for product in products]

    gated = None
    for chunk in range(CHUNKS):
        gated, state = scan_gate(
            chunk,
            turn,
            norms[chunk],
            conv_outs[chunk],
            gate_z,
            dt_weight,
            dt_bias,
            a_log,
            skip_gain,
            state,
            gated,
        )

    final_rows = state[picked_rows].astype(jnp.bfloat16)
    final_got = exchange([final_rows[k] for k in range(groups)])
    new_ssm = ssm_cache.at[targets].set(
        jnp.concatenate(final_got, axis=0).astype(jnp.float32), mode="drop"
    )
    return (gated, new_ssm, new_conv)


def solution(mesh):
    placed = (
        P("dp", None, "tensor"),
        P("dp", None, "tensor"),
        P(None, "tensor"),
        P("tensor"),
        P("tensor", None),
        P(None, "tensor"),
        P("tensor"),
        P(None, "tensor"),
        P("tensor"),
        P("dp", None, "tensor"),
        P("dp", None, "tensor"),
        P(),
        P(),
    )
    return jax.shard_map(
        body,
        mesh=mesh,
        in_specs=placed,
        out_specs=(P("dp", None, "tensor"), P("dp", None, "tensor"), P("dp", None, "tensor")),
        check_vma=False,
    )
```
